32 devices in a mesh: dp: 4 (over z), ctx: 2 (over x), tp: 4 (over y, core).
Axes of the slice: x: 2, y: 2, z: 4, core: 2. Of those that a mesh axis runs over, the one named last changes fastest.
Arguments:
- tokens: bfloat16 [8, 1024, 2048], P('dp', 'ctx'), may hold values from -6 to 6
- positions: int32 [8, 1024], P('dp', 'ctx'), may hold values from 0 to 3069, as said below
- block_ids: int32 [8, 1024], P('dp', 'ctx'), may hold values from 0 to 7, never falling along the last dimension, each value on 1 to 256 neighbouring positions
- attn_gain: bfloat16 [2048], P(('dp', 'ctx')), may hold values from 0.5 to 1.5
- w_query: bfloat16 [2048, 2048], P(('dp', 'ctx'), 'tp'), may hold values from -0.125 to 0.125
- w_key: bfloat16 [2048, 1024], P(('dp', 'ctx'), 'tp'), may hold values from -0.125 to 0.125
- w_value: bfloat16 [2048, 1024], P(('dp', 'ctx'), 'tp'), may hold values from -0.125 to 0.125
- w_out: bfloat16 [2048, 2048], P('tp', ('dp', 'ctx')), may hold values from -1 to 1
- query_gain: bfloat16 [128], replicated, may hold values from 0.5 to 1.5
- key_gain: bfloat16 [128], replicated, may hold values from 0.5 to 1.5
- mlp_gain: bfloat16 [2048], P(('dp', 'ctx')), may hold values from 0.5 to 1.5
- w_gate: bfloat16 [2048, 6144], P(('dp', 'ctx'), 'tp'), may hold values from -0.125 to 0.125
- w_up: bfloat16 [2048, 6144], P(('dp', 'ctx'), 'tp'), may hold values from -0.125 to 0.125
- w_down: bfloat16 [6144, 2048], P('tp', ('dp', 'ctx')), may hold values from -0.078125 to 0.078125
- cotangent: bfloat16 [8, 1024, 2048], P('dp', 'ctx'), may hold values from -6 to 6
Outputs:
- layer_output: bfloat16 [8, 1024, 2048], P('dp', 'ctx')
- input_grad: float32 [8, 1024, 2048], P('dp', 'ctx')
- grad_attn_gain: float32 [2048], P(('dp', 'ctx'))
- grad_w_query: float32 [2048, 2048], P(('dp', 'ctx'), 'tp')
- grad_w_key: float32 [2048, 1024], P(('dp', 'ctx'), 'tp')
- grad_w_value: float32 [2048, 1024], P(('dp', 'ctx'), 'tp')
- grad_w_out: float32 [2048, 2048], P('tp', ('dp', 'ctx'))
- grad_query_gain: float32 [128], replicated
- grad_key_gain: float32 [128], replicated
- grad_mlp_gain: float32 [2048], P(('dp', 'ctx'))
- grad_w_gate: float32 [2048, 6144], P(('dp', 'ctx'), 'tp')
- grad_w_up: float32 [2048, 6144], P(('dp', 'ctx'), 'tp')
- grad_w_down: float32 [6144, 2048], P('tp', ('dp', 'ctx'))
The draws below stay inside these ranges and needn't reach their ends.
Inputs may be any that keep to these rules, and one draw needn't show every extreme that they name: Within each sequence positions start at 0 and rise by 1 to 3 from each token to the next; the first sequence rises by 3 at every token. `block_ids`: within each sequence block ids start at 0, never fall, rise by at most one from token to token and reach 7; a block holds 1 to 256 tokens.
All inputs are finite; a program needn't handle non-finite values.
Results may differ from the reference program's by a relative error of at most 0.023.
Values may be sent and summed in bfloat16 or wider, within the bound.
No kernel may reach another device: no remote copies, remote signals or barrier semaphores. Data moves between devices by JAX's collectives and lax.ppermute only.
A program may use at most 256 MiB of HBM per device.

```python
import math
import jax
import jax.numpy as jnp
import numpy as np
from jax import lax

D = 2048
HQ = 16
KVH = 8
HD = 128
FF = 6144
BLOCK = 128
LENGTH = 1024
SEQS = 8


def draw_positions(key, part):
    increments = jax.random.randint(key, (SEQS, LENGTH), 1, 4)
    increments = increments.at[0].set(3)
    rising = jnp.cumsum(increments, axis=1) - increments[:, :1]
    return rising.astype(jnp.int32)


def block_levels(rng, dims, shards, smallest, largest):
    gain, own = 1.0, jax.random.fold_in(rng, 6)
    for axis_at, parts in shards:
        draws = jnp.exp(jax.random.uniform(jax.random.fold_in(own, axis_at), (parts,), jnp.float32, smallest / len(shards), largest / len(shards)))
        gain = gain * jnp.repeat(draws, dims[axis_at] // parts).reshape([-1 if axis == axis_at else 1 for axis in range(len(dims))])
    return gain


def length_profile(number_of, total, bound, skew):
    loads = [(1 << 20) // math.isqrt(rank ** skew) + 1 for rank in range(2, number_of + 1)]
    surplus, given = total - bound - (number_of - 1), [1] * (number_of - 1)
    while surplus > 0:
        candidates = [i for i in range(number_of - 1) if given[i] < bound]
        pool, left = sum([loads[i] for i in candidates]), surplus
        for i in candidates:
            extra = min(bound - given[i], max(1, left * loads[i] // pool), surplus)
            given[i] = given[i] + extra
            surplus = surplus - extra
    return np.array([bound] + given)


def ragged(own_key, count, total, limit, lean):
    if count == 2:
        one = jax.random.randint(own_key, (), max(1, total - limit), min(limit, total - 1) + 1)
        return jnp.stack([one, total - one])
    sizes = jnp.asarray(length_profile(count, total, limit, lean), jnp.int32)
    couples = (count - 1) // 2
    source_of, taker = sizes[1:1 + 2 * couples:2], sizes[2:2 + 2 * couples:2]
    margin = jnp.minimum(source_of - 1, limit - taker)
    passed = jax.random.randint(jax.random.fold_in(own_key, 1), (couples,), 0, 1 << 20) % (margin + 1)
    sizes = sizes.at[1:1 + 2 * couples:2].set(source_of - passed).at[2:2 + 2 * couples:2].set(taker + passed)
    return sizes[jax.random.permutation(jax.random.fold_in(own_key, 2), count)]


def bell_draw(stream_key, extent, width, limit, cuts=(), kind=jnp.bfloat16):
    entries = width * jax.random.normal(stream_key, extent, jnp.float32)
    if cuts:
        entries = entries * block_levels(stream_key, extent, cuts, -0.22, 0.18)
    return jnp.clip(entries, -limit, limit).astype(kind)


def setup_inputs(seed: int = 0) -> dict:
    splits = jax.random.split(jax.random.key(seed), 16)
    tokens = bell_draw(splits[0], (SEQS, LENGTH, D), 1.0, 6.0, ((0, 4), (1, 2)))
    positions = draw_positions(jax.random.fold_in(splits[15], 71), 0)
    block_ids = jax.vmap(lambda own: jnp.searchsorted(jnp.cumsum(ragged(own, LENGTH // BLOCK, LENGTH, 2 * BLOCK, 1)), jnp.arange(LENGTH), side="right"))(jax.random.split(splits[2], SEQS)).reshape((SEQS, LENGTH)).astype(jnp.int32)
    attn_gain = jnp.clip(1.0 + 0.1 * jax.random.normal(splits[3], (D,), jnp.float32), 0.5, 1.5).astype(jnp.bfloat16)
    w_query = bell_draw(splits[4], (D, HQ * HD), D ** -0.5, 0.125, ((0, 8), (1, 4)))
    w_key = bell_draw(splits[5], (D, KVH * HD), D ** -0.5, 0.125, ((0, 8), (1, 4)))
    w_value = bell_draw(splits[6], (D, KVH * HD), D ** -0.5, 0.125, ((0, 8), (1, 4)))
    w_out = bell_draw(splits[7], (HQ * HD, D), (HQ * HD // 64) ** -0.5, 1.0, ((0, 4), (1, 8)))
    query_gain = jnp.clip(1.0 + 0.1 * jax.random.normal(splits[8], (HD,), jnp.float32), 0.5, 1.5).astype(jnp.bfloat16)
    key_gain = jnp.clip(1.0 + 0.1 * jax.random.normal(splits[9], (HD,), jnp.float32), 0.5, 1.5).astype(jnp.bfloat16)
    mlp_gain = jnp.clip(1.0 + 0.1 * jax.random.normal(splits[10], (D,), jnp.float32), 0.5, 1.5).astype(jnp.bfloat16)
    w_gate = bell_draw(splits[11], (D, FF), D ** -0.5, 0.125, ((0, 8), (1, 4)))
    w_up = bell_draw(splits[12], (D, FF), D ** -0.5, 0.125, ((0, 8), (1, 4)))
    w_down = bell_draw(splits[13], (FF, D), FF ** -0.5, 0.078125, ((0, 4), (1, 8)))
    cotangent = bell_draw(splits[14], (SEQS, LENGTH, D), 1.0, 6.0, ((0, 4), (1, 2)))
    return dict(tokens=tokens, positions=positions, block_ids=block_ids, attn_gain=attn_gain, w_query=w_query, w_key=w_key, w_value=w_value, w_out=w_out, query_gain=query_gain, key_gain=key_gain, mlp_gain=mlp_gain, w_gate=w_gate, w_up=w_up, w_down=w_down, cotangent=cotangent)


EPS = 1e-06
THETA = 1000000.0
NEG = -1e+30
HIGH = lax.Precision.HIGHEST

@jax.custom_vjp
def low(v):
    return lax.optimization_barrier(v.astype(jnp.bfloat16)).astype(jnp.float32)

@jax.custom_vjp
def low_back(v):
    return v

def low_keep(v):
    return (low(v), None)

def low_pass(kept, grad):
    return (grad,)

def back_keep(v):
    return (v, None)

def back_low(kept, grad):
    return (low(grad),)
low.defvjp(low_keep, low_pass)
low_back.defvjp(back_keep, back_low)

def root_norm(values, gain_row):
    return values * lax.rsqrt(lax.optimization_barrier(jnp.mean(values * values, axis=-1, keepdims=True)) + EPS) * gain_row

def rotate(values, places):
    half_dim = values.shape[-1] // 2
    exponent = jnp.arange(half_dim, dtype=jnp.float32) * (2.0 / values.shape[-1])
    inverse = jnp.power(THETA, -exponent)
    angle = places.astype(jnp.float32)[:, None] * inverse[None, :]
    cosine_rows = jnp.cos(angle)[:, None, :]
    sine_rows = jnp.sin(angle)[:, None, :]
    first = values[..., :half_dim]
    second = values[..., half_dim:]
    return jnp.concatenate([first * cosine_rows - second * sine_rows, second * cosine_rows + first * sine_rows], axis=-1)

def product(left, right):
    return jnp.dot(left, right, precision=HIGH, preferred_element_type=jnp.float32)

def forward_seq(inputs, params, places, blocks):
    attn_gain, w_query, w_key, w_value, w_out, query_gain, key_gain, mlp_gain, w_gate, w_up, w_down = params
    length = inputs.shape[0]
    head_dim = query_gain.shape[0]
    head_count = w_query.shape[1] // head_dim
    kv_count = w_key.shape[1] // head_dim
    group_size = head_count // kv_count
    normed = low(root_norm(inputs, attn_gain))
    query = low_back(product(normed, w_query)).reshape(length, head_count, head_dim)
    query = low(rotate(root_norm(query, query_gain), places))
    keys = low_back(product(normed, w_key)).reshape(length, kv_count, head_dim)
    keys = low(rotate(root_norm(keys, key_gain), places))
    values = low(low_back(product(normed, w_value))).reshape(length, kv_count, head_dim)
    row_block = math.gcd(512, length)
    block_count = length // row_block
    grouped = query.reshape(block_count, row_block, kv_count, group_size, head_dim)

    def attend(data):
        query_rows, row_ids = data
        raw = jnp.einsum('qkgd,tkd->kgqt', query_rows, keys, precision=HIGH, preferred_element_type=jnp.float32)
        scores = low_back(raw) * head_dim ** (-0.5)
        allowed = blocks[None, :] <= row_ids[:, None]
        scores = jnp.where(allowed, scores, NEG)
        top_score = lax.optimization_barrier(jnp.max(scores, axis=-1, keepdims=True))
        weights = jnp.exp(scores - top_score)
        weights = low(weights / lax.optimization_barrier(jnp.sum(weights, axis=-1, keepdims=True)))
        mixed = jnp.einsum('kgqt,tkd->qkgd', weights, values, precision=HIGH, preferred_element_type=jnp.float32)
        return low(low_back(mixed))
    attended = lax.map(jax.checkpoint(attend), (grouped, blocks.reshape(block_count, row_block)))
    attended = attended.reshape(length, head_count * head_dim)
    hidden = inputs + low_back(product(attended, w_out))
    normed_two = low(root_norm(hidden, mlp_gain))
    gate = low_back(product(normed_two, w_gate))
    upper = low_back(product(normed_two, w_up))
    active = low(jax.nn.silu(gate) * upper)
    return hidden + low_back(product(active, w_down))

def reference(tokens, positions, block_ids, attn_gain, w_query, w_key, w_value, w_out, query_gain, key_gain, mlp_gain, w_gate, w_up, w_down, cotangent):
    params = tuple((weight.astype(jnp.float32) for weight in (attn_gain, w_query, w_key, w_value, w_out, query_gain, key_gain, mlp_gain, w_gate, w_up, w_down)))

    def per_sequence(totals, data):
        inputs, places, blocks, grad_out = data

        def forward(values, *weights):
            return forward_seq(values, weights, places, blocks)
        output, pull = jax.vjp(forward, inputs.astype(jnp.float32), *params)
        grads = pull(grad_out.astype(jnp.float32))
        totals = tuple((total_part + grad_part for total_part, grad_part in zip(totals, grads[1:])))
        return (totals, (output.astype(jnp.bfloat16), grads[0]))
    initial = tuple((jnp.zeros(weight.shape, jnp.float32) for weight in params))
    totals, (outputs, input_grads) = lax.scan(per_sequence, initial, (tokens, positions, block_ids, cotangent))
    return (outputs, input_grads, totals[0], totals[1], totals[2], totals[3], totals[4], totals[5], totals[6], totals[7], totals[8], totals[9], totals[10])
```

```python
import functools

import jax
import jax.numpy as jnp
from jax import lax
from jax.experimental import pallas as pl
from jax.experimental.pallas import tpu as pltpu
from jax.sharding import PartitionSpec as P

EPS = 1e-06
THETA = 1000000.0
LOG2E = 1.4426950408889634
ROWS_CONTRACT = (((0,), (0,)), ((), ()))
COLS_CONTRACT = (((1,), (1,)), ((), ()))
BF16 = jnp.bfloat16
F32 = jnp.float32


def over_rows(left, right):
    return lax.dot_general(left, right, ROWS_CONTRACT, preferred_element_type=F32)


def against(left, right):
    return lax.dot_general(left, right, COLS_CONTRACT, preferred_element_type=F32)


def matmul(left, right):
    return jnp.dot(left, right, preferred_element_type=F32)


def ring(size, shift):
    return [(i, (i + shift) % size) for i in range(size)]


def after(value, *others):
    return lax.optimization_barrier((value, *others))[0]


def project_body(tok, gain, w, cos, sin, gq, gk, normed, raw, qkv, *, heads, kv_heads, dim):
    x = tok[...].astype(F32)
    r = lax.rsqrt(jnp.mean(x * x, axis=-1, keepdims=True) + EPS)
    n = (x * r * gain[...].astype(F32)).astype(BF16)
    normed[...] = n
    y = jnp.dot(n, w[...], preferred_element_type=F32)
    cosine = cos[...]
    sine = sin[...]
    for h in range(heads + kv_heads):
        v = y[:, h * dim : (h + 1) * dim]
        raw[:, h * dim : (h + 1) * dim] = v
        g = (gq if h < heads else gk)[...].astype(F32)
        nv = v * lax.rsqrt(jnp.mean(v * v, axis=-1, keepdims=True) + EPS) * g
        out = nv * cosine + pltpu.roll(nv, dim // 2, axis=1) * sine
        qkv[:, h * dim : (h + 1) * dim] = out.astype(BF16)
    start = (heads + kv_heads) * dim
    qkv[:, start:] = y[:, start:].astype(BF16)


def project(tok, gain, w, cos, sin, gq, gk, heads, kv_heads, dim):
    rows, width = tok.shape
    out_width = w.shape[1]
    raw_width = (heads + kv_heads) * dim
    block = min(256, rows)
    row = lambda cols: pl.BlockSpec((block, cols), lambda i: (i, 0))
    full = lambda a: pl.BlockSpec(a.shape, lambda i: (0, 0))
    return pl.pallas_call(
        functools.partial(project_body, heads=heads, kv_heads=kv_heads, dim=dim),
        grid=(rows // block,),
        in_specs=[row(width), full(gain), full(w), row(dim), row(dim), full(gq), full(gk)],
        out_specs=[row(width), row(raw_width), row(out_width)],
        out_shape=[
            jax.ShapeDtypeStruct((rows, width), BF16),
            jax.ShapeDtypeStruct((rows, raw_width), F32),
            jax.ShapeDtypeStruct((rows, out_width), BF16),
        ],
        name="project",
    )(tok, gain, w, cos, sin, gq, gk)


def attend_body(q, k, v, qid, kid, out, *, scale):
    s = lax.dot_general(q[0], k[0], COLS_CONTRACT, preferred_element_type=F32)
    e = jnp.where(kid[0] <= qid[0], jnp.exp2(s * (scale * LOG2E)), 0.0)
    total = jnp.sum(e, axis=-1, keepdims=True)
    o = jnp.dot((e * (1.0 / total)).astype(BF16), v[0], preferred_element_type=F32)
    out[0] = o.astype(BF16)


def attend(qkv, keys, qid_col, kid_row, heads, kv_heads, dim):
    batch, rows, _ = qkv.shape
    length = keys.shape[1]
    group = heads // kv_heads
    block = max(128, min(rows, rows * 1024 // length))
    return pl.pallas_call(
        functools.partial(attend_body, scale=dim**-0.5),
        grid=(batch, heads, rows // block),
        in_specs=[
            pl.BlockSpec((1, block, dim), lambda b, h, i: (b, i, h)),
            pl.BlockSpec((1, length, dim), lambda b, h, i: (b, 0, h // group)),
            pl.BlockSpec((1, length, dim), lambda b, h, i: (b, 0, kv_heads + h // group)),
            pl.BlockSpec((1, block, 1), lambda b, h, i: (b, i, 0)),
            pl.BlockSpec((1, 1, length), lambda b, h, i: (b, 0, 0)),
        ],
        out_specs=pl.BlockSpec((1, block, dim), lambda b, h, i: (b, i, h)),
        out_shape=jax.ShapeDtypeStruct((batch, rows, heads * dim), BF16),
        name="attend",
    )(qkv, keys, keys, qid_col, kid_row)


def attend_back_body(q, k, v, go, qid, kid, dq, dk, dv, *, scale):
    @pl.when((pl.program_id(2) == 0) & (pl.program_id(3) == 0))
    def _():
        dk[...] = jnp.zeros_like(dk)
        dv[...] = jnp.zeros_like(dv)

    s = lax.dot_general(k[0], q[0], COLS_CONTRACT, preferred_element_type=F32)
    e = jnp.where(kid[0] <= qid[0], jnp.exp2(s * (scale * LOG2E)), 0.0)
    p = e * (1.0 / jnp.sum(e, axis=0, keepdims=True))
    gp = lax.dot_general(v[0], go[0], COLS_CONTRACT, preferred_element_type=F32)
    delta = jnp.sum(p * gp, axis=0, keepdims=True)
    gs = (p * (gp - delta)).astype(BF16)
    dv[0] += jnp.dot(p.astype(BF16), go[0], preferred_element_type=F32)
    dk[0] += jnp.dot(gs, q[0], preferred_element_type=F32) * scale
    dq[0] = lax.dot_general(gs, k[0], ROWS_CONTRACT, preferred_element_type=F32) * scale


def attend_back(qkv, keys, go, qid_row, kid_col, heads, kv_heads, dim):
    batch, rows, _ = qkv.shape
    length = keys.shape[1]
    group = heads // kv_heads
    block = max(128, min(rows, rows * 1024 // length))
    head = lambda h, g: h * group + g
    return pl.pallas_call(
        functools.partial(attend_back_body, scale=dim**-0.5),
        grid=(batch, kv_heads, group, rows // block),
        in_specs=[
            pl.BlockSpec((1, block, dim), lambda b, h, g, i: (b, i, head(h, g))),
            pl.BlockSpec((1, length, dim), lambda b, h, g, i: (b, 0, h)),
            pl.BlockSpec((1, length, dim), lambda b, h, g, i: (b, 0, kv_heads + h)),
            pl.BlockSpec((1, block, dim), lambda b, h, g, i: (b, i, head(h, g))),
            pl.BlockSpec((1, 1, block), lambda b, h, g, i: (b, 0, i)),
            pl.BlockSpec((1, length, 1), lambda b, h, g, i: (b, 0, 0)),
        ],
        out_specs=[
            pl.BlockSpec((1, block, dim), lambda b, h, g, i: (b, i, head(h, g))),
            pl.BlockSpec((1, length, dim), lambda b, h, g, i: (b, 0, h)),
            pl.BlockSpec((1, length, dim), lambda b, h, g, i: (b, 0, h)),
        ],
        out_shape=[
            jax.ShapeDtypeStruct((batch, rows, heads * dim), F32),
            jax.ShapeDtypeStruct((batch, length, kv_heads * dim), F32),
            jax.ShapeDtypeStruct((batch, length, kv_heads * dim), F32),
        ],
        name="attend_back",
    )(qkv, keys, keys, go, qid_row, kid_col)


def heads_back_body(dq, dk, dv, raw, cos, sin, gq, gk, out, sums, *, heads, kv_heads, dim):
    @pl.when(pl.program_id(0) == 0)
    def _():
        sums[...] = jnp.zeros_like(sums)

    cosine = cos[...]
    sine = sin[...]
    for h in range(heads + kv_heads):
        is_query = h < heads
        g = dq[:, h * dim : (h + 1) * dim] if is_query else dk[:, (h - heads) * dim : (h - heads + 1) * dim]
        gain = (gq if is_query else gk)[...].astype(F32)
        v = raw[:, h * dim : (h + 1) * dim]
        r = lax.rsqrt(jnp.mean(v * v, axis=-1, keepdims=True) + EPS)
        unit = v * r
        gn = g * cosine + pltpu.roll(g * sine, dim // 2, axis=1)
        line = 0 if is_query else 1
        sums[line : line + 1, :] += jnp.sum(gn * unit, axis=0, keepdims=True)
        e = gn * gain
        back = r * (e - unit * jnp.mean(e * unit, axis=-1, keepdims=True))
        out[:, h * dim : (h + 1) * dim] = back.astype(BF16)
    out[:, (heads + kv_heads) * dim :] = dv[...].astype(BF16)


def heads_back(dq, dk, dv, raw, cos, sin, gq, gk, heads, kv_heads, dim):
    rows = dq.shape[0]
    block = min(256, rows)
    width = (heads + 2 * kv_heads) * dim
    row = lambda a: pl.BlockSpec((block, a.shape[1]), lambda i: (i, 0))
    full = lambda a: pl.BlockSpec(a.shape, lambda i: (0, 0))
    return pl.pallas_call(
        functools.partial(heads_back_body, heads=heads, kv_heads=kv_heads, dim=dim),
        grid=(rows // block,),
        in_specs=[row(dq), row(dk), row(dv), row(raw), row(cos), row(sin), full(gq), full(gk)],
        out_specs=[
            pl.BlockSpec((block, width), lambda i: (i, 0)),
            pl.BlockSpec((8, dim), lambda i: (0, 0)),
        ],
        out_shape=[
            jax.ShapeDtypeStruct((rows, width), BF16),
            jax.ShapeDtypeStruct((8, dim), F32),
        ],
        name="heads_back",
    )(dq, dk, dv, raw, cos, sin, gq, gk)


def shards(
    tokens,
    positions,
    block_ids,
    attn_gain,
    w_query,
    w_key,
    w_value,
    w_out,
    query_gain,
    key_gain,
    mlp_gain,
    w_gate,
    w_up,
    w_down,
    cotangent,
    *,
    sizes,
):
    dp_n, ctx_n, tp_n = sizes
    dp_at, ctx_at, tp_at = (lax.axis_index(name) for name in ("dp", "ctx", "tp"))
    batch, shard_len, model = tokens.shape
    rows = batch * shard_len
    dim = query_gain.shape[0]
    heads = w_query.shape[1] // dim
    kv_heads = w_key.shape[1] // dim
    piece = w_query.shape[0]
    hidden_width = w_gate.shape[1]
    attn_width = w_query.shape[1]

    def spread(own):
        got = []
        for s in range(dp_n):
            held = lax.ppermute(own, "dp", ring(dp_n, s)) if s else own
            for t in range(ctx_n):
                if t:
                    held = lax.ppermute(held, "ctx", ring(ctx_n, 1))
                got.append((lax.rem(dp_at + dp_n - s, dp_n), lax.rem(ctx_at + ctx_n - t, ctx_n), held))
        return got

    def place(target, got, column, take=lambda a: a):
        for d, c, held in got:
            target = lax.dynamic_update_slice(target, take(held)[None, None], (d, c, 0, column))
        return target

    def empty(width, depth=piece):
        return jnp.zeros((dp_n, ctx_n, depth, width), BF16)

    gains = jnp.concatenate([attn_gain, mlp_gain])
    qkv_local = jnp.concatenate([w_query, w_key, w_value], axis=1)
    extra = 8
    packed_gains = jnp.pad(gains[None, :], ((0, extra - 1), (0, qkv_local.shape[1] - gains.shape[0])))
    pack_one = jnp.concatenate([qkv_local, packed_gains], axis=0)
    got_one = spread(pack_one)
    pack_out = after(w_out.T, got_one[ctx_n][2])
    got_out = spread(pack_out)
    pack_gate = after(w_gate, got_out[ctx_n][2])
    got_gate = spread(pack_gate)
    pack_up = after(w_up, got_gate[ctx_n][2])
    got_up = spread(pack_up)
    pack_down = after(w_down.T, got_up[ctx_n][2])
    got_down = spread(pack_down)

    qkv_w = place(empty(qkv_local.shape[1]), got_one, 0, lambda a: a[:piece]).reshape(model, -1)
    gain_table = place(empty(2 * piece, 1), got_one, 0, lambda a: a[piece : piece + 1, : 2 * piece])
    gain_table = gain_table.reshape(dp_n * ctx_n, 2, piece)
    gain_one = gain_table[:, 0, :].reshape(1, model)
    gain_two = gain_table[:, 1, :].reshape(1, model).astype(F32)
    out_w = place(empty(attn_width), got_out, 0).reshape(model, attn_width)
    both = empty(2 * hidden_width)
    both = place(place(both, got_gate, 0), got_up, hidden_width)
    both_w = both.reshape(model, 2 * hidden_width)
    down_w = place(empty(hidden_width), got_down, 0).reshape(model, hidden_width)

    bits = []
    while (1 << len(bits)) < tp_n:
        bits.append(1 << len(bits))

    def swap(value, bit):
        return lax.ppermute(value, "tp", [(i, i ^ bit) for i in range(tp_n)])

    def fold(partial):
        for bit in bits:
            half = partial.shape[0] // 2
            up = jnp.bitwise_and(tp_at // bit, 1)
            sent = lax.dynamic_slice_in_dim(partial, (1 - up) * half, half, 0)
            kept = lax.dynamic_slice_in_dim(partial, up * half, half, 0)
            partial = kept.astype(F32) + swap(sent.astype(BF16), bit).astype(F32)
            if bit != bits[-1]:
                partial = partial.astype(BF16)
        return partial

    quarter = rows // tp_n

    def offset(rank):
        at, size = 0, rows
        for bit in bits:
            size //= 2
            at = at + jnp.bitwise_and(rank // bit, 1) * size
        return at

    def own_rows(value):
        return lax.dynamic_slice_in_dim(value, offset(tp_at), quarter, 0)

    def unfold(own):
        held = [(0, own)]
        for bit in reversed(bits):
            held = held + [(mask | bit, swap(value, bit)) for mask, value in held]
        whole = jnp.zeros((rows,) + own.shape[1:], own.dtype)
        for mask, value in held:
            whole = lax.dynamic_update_slice_in_dim(whole, value, offset(jnp.bitwise_xor(tp_at, mask)), 0)
        return whole

    flat_tokens = tokens.reshape(rows, model)
    flat_cotangent = cotangent.reshape(rows, model)
    exponent = jnp.arange(dim // 2, dtype=F32) * (2.0 / dim)
    angle = positions.reshape(rows, 1).astype(F32) * jnp.power(THETA, -exponent)[None, :]
    cosine, sine = jnp.cos(angle), jnp.sin(angle)
    cosine = jnp.concatenate([cosine, cosine], axis=1)
    sine = jnp.concatenate([-sine, sine], axis=1)
    gain_q, gain_k = query_gain[None, :], key_gain[None, :]

    def around(value):
        held = [value]
        for _ in range(ctx_n - 1):
            held.append(lax.ppermute(held[-1], "ctx", ring(ctx_n, 1)))
        return jnp.concatenate(held, axis=1)

    key_ids = around(block_ids)
    normed, raw, qkv = project(
        flat_tokens, gain_one, qkv_w, cosine, sine, gain_q, gain_k, heads, kv_heads, dim
    )
    qkv = qkv.reshape(batch, shard_len, -1)
    keys = around(qkv[:, :, attn_width:])
    attended = attend(
        qkv, keys, block_ids[:, :, None], key_ids[:, None, :], heads, kv_heads, dim
    ).reshape(rows, attn_width)
    branch = fold(against(attended, out_w).astype(BF16))
    hidden = own_rows(flat_tokens).astype(F32) + branch

    root_two = lax.rsqrt(jnp.mean(hidden * hidden, axis=-1, keepdims=True) + EPS)
    unit_two = hidden * root_two
    normed_two = unfold((unit_two * gain_two).astype(BF16))
    gate = matmul(normed_two, both_w[:, :hidden_width])
    upper = matmul(normed_two, both_w[:, hidden_width:])
    sigmoid = jax.nn.sigmoid(gate)
    active = (gate * sigmoid * upper).astype(BF16)

    def share(full):
        parts = full.reshape(dp_n, ctx_n, piece, full.shape[1])

        def block(d, c):
            return lax.dynamic_slice(parts, (d, c, 0, 0), (1, 1, piece, full.shape[1]))[0, 0]

        def over_ctx(d):
            held = block(d, lax.rem(ctx_at + ctx_n - 1, ctx_n))
            for t in range(1, ctx_n):
                got = lax.ppermute(held, "ctx", ring(ctx_n, 1)).astype(F32)
                held = block(d, lax.rem(ctx_at + 2 * ctx_n - 1 - t, ctx_n)).astype(F32) + got
                if t < ctx_n - 1:
                    held = held.astype(BF16)
            return held

        arrived = []
        for s in range(1, dp_n):
            sent = over_ctx(lax.rem(dp_at + s, dp_n)).astype(BF16)
            arrived.append(lax.ppermute(sent, "dp", ring(dp_n, s)))
        total = over_ctx(dp_at)
        for part in arrived:
            total = total + part.astype(F32)
        return total

    grad_down = share(over_rows(flat_cotangent, active).astype(BF16))
    g_active = matmul(flat_cotangent, down_w)
    result = hidden + fold(against(active, down_w).astype(BF16))
    layer_output = unfold(result.astype(BF16)).reshape(batch, shard_len, model)
    g_gate = (g_active * upper * sigmoid * (1.0 + gate * (1.0 - sigmoid))).astype(BF16)
    g_up = (g_active * (gate * sigmoid)).astype(BF16)
    g_both = jnp.concatenate([g_gate, g_up], axis=1)
    g_normed_two = fold(against(g_both, both_w).astype(BF16))
    grad_gate = share(over_rows(normed_two, g_gate).astype(BF16))
    grad_up = share(over_rows(normed_two, g_up).astype(BF16))
    e_two = g_normed_two * gain_two
    g_hidden = own_rows(flat_cotangent).astype(F32) + root_two * (
        e_two - unit_two * jnp.mean(e_two * unit_two, axis=-1, keepdims=True)
    )
    mlp_gain_sum = jnp.sum(g_normed_two * unit_two, axis=0)

    g_branch = unfold(g_hidden.astype(BF16))
    g_attended = matmul(g_branch, out_w).astype(BF16).reshape(batch, shard_len, attn_width)
    grad_out = share(over_rows(g_branch, attended).astype(BF16))
    dq, dk, dv = attend_back(
        qkv, keys, g_attended, block_ids[:, None, :], key_ids[:, :, None], heads, kv_heads, dim
    )

    def home(value):
        parts = [value[:, i * shard_len : (i + 1) * shard_len] for i in range(ctx_n)]
        held = parts[1 % ctx_n]
        for t in range(1, ctx_n):
            got = lax.ppermute(held.astype(BF16), "ctx", ring(ctx_n, 1)).astype(F32)
            held = parts[(t + 1) % ctx_n] + got
        return held.reshape(rows, -1)

    g_raw, gain_sums = heads_back(
        dq.reshape(rows, attn_width), home(dk), home(dv), raw, cosine, sine, gain_q, gain_k, heads, kv_heads, dim
    )
    g_normed = fold(against(g_raw, qkv_w).astype(BF16))
    grad_qkv = share(over_rows(normed, g_raw).astype(BF16))
    own_tokens = own_rows(flat_tokens).astype(F32)
    root_one = lax.rsqrt(jnp.mean(own_tokens * own_tokens, axis=-1, keepdims=True) + EPS)
    unit_one = own_tokens * root_one
    e_one = g_normed * gain_one.astype(F32)
    input_own = g_hidden + root_one * (
        e_one - unit_one * jnp.mean(e_one * unit_one, axis=-1, keepdims=True)
    )
    input_grad = unfold(input_own.astype(BF16)).astype(F32).reshape(batch, shard_len, model)
    attn_gain_sum = jnp.sum(g_normed * unit_one, axis=0)

    small = jnp.concatenate([mlp_gain_sum, attn_gain_sum, gain_sums[0], gain_sums[1]])
    small = small.reshape(-1, dim)
    for name, size in (("tp", tp_n), ("ctx", ctx_n), ("dp", dp_n)):
        bit = 1
        while bit < size:
            small = small + lax.ppermute(small, name, [(i, i ^ bit) for i in range(size)])
            bit *= 2
    small = small.reshape(-1)
    start = (dp_at * ctx_n + ctx_at) * piece
    grad_mlp_gain = lax.dynamic_slice_in_dim(small, start, piece, 0)
    grad_attn_gain = lax.dynamic_slice_in_dim(small, model + start, piece, 0)
    grad_query_gain = small[2 * model : 2 * model + dim]
    grad_key_gain = small[2 * model + dim :]

    kv_width = kv_heads * dim
    return (
        layer_output,
        input_grad,
        grad_attn_gain,
        grad_qkv[:, :attn_width],
        grad_qkv[:, attn_width : attn_width + kv_width],
        grad_qkv[:, attn_width + kv_width :],
        grad_out.T,
        grad_query_gain,
        grad_key_gain,
        grad_mlp_gain,
        grad_gate,
        grad_up,
        grad_down.T,
    )


def solution(mesh):
    rows_split = P(("dp", "ctx"), "tp")
    cols_split = P("tp", ("dp", "ctx"))
    vector = P(("dp", "ctx"))
    tokens = P("dp", "ctx", None)
    return jax.shard_map(
        functools.partial(shards, sizes=tuple(mesh.shape[name] for name in ("dp", "ctx", "tp"))),
        mesh=mesh,
        in_specs=(
            tokens,
            P("dp", "ctx"),
            P("dp", "ctx"),
            vector,
            rows_split,
            rows_split,
            rows_split,
            cols_split,
            P(),
            P(),
            vector,
            rows_split,
            rows_split,
            cols_split,
            tokens,
        ),
        out_specs=(
            tokens,
            tokens,
            vector,
            rows_split,
            rows_split,
            rows_split,
            cols_split,
            P(),
            P(),
            vector,
            rows_split,
            rows_split,
            cols_split,
        ),
        check_vma=False,
    )
```

```python
import functools

import jax
import jax.numpy as jnp
from jax import lax
from jax.experimental import pallas as pl
from jax.experimental.pallas import tpu as pltpu
from jax.sharding import PartitionSpec as P


EPS = 1e-06
THETA = 1000000.0
LOG2E = 1.4426950408889634
ROWS_CONTRACT = (((0,), (0,)), ((), ()))
COLS_CONTRACT = (((1,), (1,)), ((), ()))
BF16 = jnp.bfloat16
F32 = jnp.float32


def over_rows(left, right):
    return lax.dot_general(left, right, ROWS_CONTRACT, preferred_element_type=F32)


def against(left, right):
    return lax.dot_general(left, right, COLS_CONTRACT, preferred_element_type=F32)


def matmul(left, right):
    return jnp.dot(left, right, preferred_element_type=F32)


def joined(pieces, axis=0):
    return lax.optimization_barrier(jnp.concatenate(pieces, axis=axis))


def ring(size):
    return [(i, (i + 1) % size) for i in range(size)]


CTX_FIRST = ('u',)
DP_FIRST = ('U',)


def whole_spec(array):
    zeros = (0,) * array.ndim
    return pl.BlockSpec(array.shape, lambda *_: zeros, pipeline_mode=pl.Buffered(1))


def call(body, grid, table, operands, outs, scratch=()):
    out_shapes, out_specs = zip(*outs)
    return pl.pallas_call(
        body,
        grid_spec=pltpu.PrefetchScalarGridSpec(
            num_scalar_prefetch=1,
            grid=grid,
            in_specs=[spec for _, spec in operands],
            out_specs=list(out_specs),
            scratch_shapes=list(scratch),
        ),
        out_shape=list(out_shapes),
    )(table, *[array for array, _ in operands])


def shape(rows, cols, dtype):
    return jax.ShapeDtypeStruct((rows, cols), dtype)


def reorder_body(table, value, out, *, row_blocks, piece):
    for j in range(value.shape[1] // piece):
        start = pl.multiple_of(table[row_blocks + j] * piece, piece)
        out[:, j * piece : (j + 1) * piece] = value[:, pl.ds(start, piece)]


def reorder(value, table, row_blocks, piece):
    rows, cols = value.shape
    block = (rows // row_blocks, cols)
    return call(
        functools.partial(reorder_body, row_blocks=row_blocks, piece=piece),
        (row_blocks,),
        table,
        [(value, pl.BlockSpec(block, lambda i, p: (p[i], 0)))],
        [(jax.ShapeDtypeStruct(value.shape, value.dtype), pl.BlockSpec(block, lambda i, _: (i, 0)))],
    )[0]


def project_body(_, tok, gain, cos, sin, gq, gk, *refs, heads, kv_heads, dim, step, width):
    pieces, (normed, raw, qkv) = refs[:-3], refs[-3:]
    x = tok[...].astype(F32)
    r = lax.rsqrt(jnp.mean(x * x, axis=-1, keepdims=True) + EPS)
    n = (x * r * gain[...].astype(F32)).astype(BF16)
    normed[...] = n
    y = None
    for j, w in enumerate(pieces):
        part = matmul(n[:, j * step : (j + 1) * step], w[:step, :width])
        y = part if y is None else y + part
    cosine = cos[...]
    sine = sin[...]
    for h in range(heads + kv_heads):
        v = y[:, h * dim : (h + 1) * dim]
        raw[:, h * dim : (h + 1) * dim] = v
        g = (gq if h < heads else gk)[...].astype(F32)
        nv = v * lax.rsqrt(jnp.mean(v * v, axis=-1, keepdims=True) + EPS) * g
        out = nv * cosine + pltpu.roll(nv, dim // 2, axis=1) * sine
        qkv[:, h * dim : (h + 1) * dim] = out.astype(BF16)
    start = (heads + kv_heads) * dim
    qkv[:, start:] = y[:, start:].astype(BF16)


def project(table, tok, gain, cos, sin, gq, gk, pieces, step, heads, kv_heads, dim):
    rows, width = tok.shape
    out_width = (heads + 2 * kv_heads) * dim
    raw_width = (heads + kv_heads) * dim
    block = min(256, rows)
    row = lambda cols: pl.BlockSpec((block, cols), lambda i, _: (i, 0))
    return call(
        functools.partial(
            project_body, heads=heads, kv_heads=kv_heads, dim=dim, step=step, width=out_width
        ),
        (rows // block,),
        table,
        [(tok, row(width)), (gain, whole_spec(gain)), (cos, row(dim)), (sin, row(dim))]
        + [(a, whole_spec(a)) for a in (gq, gk, *pieces)],
        [
            (shape(rows, width, BF16), row(width)),
            (shape(rows, raw_width, F32), row(raw_width)),
            (shape(rows, out_width, BF16), row(out_width)),
        ],
    )


def attend_body(q, k, v, qid, kid, out, *, scale):
    s = against(q[0], k[0])
    e = jnp.where(kid[0] <= qid[0], jnp.exp2(s * (scale * LOG2E)), 0.0)
    total = jnp.sum(e, axis=-1, keepdims=True)
    out[0] = matmul((e * (1.0 / total)).astype(BF16), v[0]).astype(BF16)


def attend(qkv, keys, qid_col, kid_row, heads, kv_heads, dim):
    batch, rows, _ = qkv.shape
    length = keys.shape[1]
    group = heads // kv_heads
    block = max(128, min(rows, rows * 1024 // length))
    return pl.pallas_call(
        functools.partial(attend_body, scale=dim**-0.5),
        grid=(batch, heads, rows // block),
        in_specs=[
            pl.BlockSpec((1, block, dim), lambda b, h, i: (b, i, h)),
            pl.BlockSpec((1, length, dim), lambda b, h, i: (b, 0, h // group)),
            pl.BlockSpec((1, length, dim), lambda b, h, i: (b, 0, kv_heads + h // group)),
            pl.BlockSpec((1, block, 1), lambda b, h, i: (b, i, 0)),
            pl.BlockSpec((1, 1, length), lambda b, h, i: (b, 0, 0)),
        ],
        out_specs=pl.BlockSpec((1, block, dim), lambda b, h, i: (b, i, h)),
        out_shape=jax.ShapeDtypeStruct((batch, rows, heads * dim), BF16),
        name="attend",
    )(qkv, keys, keys, qid_col, kid_row)


def attend_back_body(q, k, v, go, qid, kid, dq, own, other, dk, dv, *, scale, kv_heads, dim):
    first = (pl.program_id(2) == 0) & (pl.program_id(3) == 0)
    last = (pl.program_id(2) == pl.num_programs(2) - 1) & (pl.program_id(3) == pl.num_programs(3) - 1)

    @pl.when(first)
    def _():
        dk[...] = jnp.zeros_like(dk)
        dv[...] = jnp.zeros_like(dv)

    s = against(k[0], q[0])
    e = jnp.where(kid[0] <= qid[0], jnp.exp2(s * (scale * LOG2E)), 0.0)
    p = e * (1.0 / jnp.sum(e, axis=0, keepdims=True))
    gp = against(v[0], go[0])
    delta = jnp.sum(p * gp, axis=0, keepdims=True)
    gs = (p * (gp - delta)).astype(BF16)
    dv[...] += matmul(p.astype(BF16), go[0])
    dk[...] += matmul(gs, q[0]) * scale
    dq[0] = over_rows(gs, k[0]) * scale

    mine = own.shape[1]
    for h in range(kv_heads):

        @pl.when(last & (pl.program_id(1) == h))
        def _():
            for total, column in ((dk, h * dim), (dv, (kv_heads + h) * dim)):
                own[0, :, column : column + dim] = total[:mine, :]
                other[0, :, column : column + dim] = total[mine:, :].astype(BF16)


def attend_back(qkv, keys, go, qid_row, kid_col, heads, kv_heads, dim):
    batch, rows, _ = qkv.shape
    length = keys.shape[1]
    group = heads // kv_heads
    block = max(128, min(rows, rows * 1024 // length))
    head = lambda h, g: h * group + g
    width = 2 * kv_heads * dim
    return pl.pallas_call(
        functools.partial(attend_back_body, scale=dim**-0.5, kv_heads=kv_heads, dim=dim),
        grid=(batch, kv_heads, group, rows // block),
        in_specs=[
            pl.BlockSpec((1, block, dim), lambda b, h, g, i: (b, i, head(h, g))),
            pl.BlockSpec((1, length, dim), lambda b, h, g, i: (b, 0, h)),
            pl.BlockSpec((1, length, dim), lambda b, h, g, i: (b, 0, kv_heads + h)),
            pl.BlockSpec((1, block, dim), lambda b, h, g, i: (b, i, head(h, g))),
            pl.BlockSpec((1, 1, block), lambda b, h, g, i: (b, 0, i)),
            pl.BlockSpec((1, length, 1), lambda b, h, g, i: (b, 0, 0)),
        ],
        out_specs=[
            pl.BlockSpec((1, block, dim), lambda b, h, g, i: (b, i, head(h, g))),
            pl.BlockSpec((1, rows, width), lambda b, h, g, i: (b, 0, 0)),
            pl.BlockSpec((1, length - rows, width), lambda b, h, g, i: (b, 0, 0)),
        ],
        out_shape=[
            jax.ShapeDtypeStruct((batch, rows, heads * dim), F32),
            jax.ShapeDtypeStruct((batch, rows, width), F32),
            jax.ShapeDtypeStruct((batch, length - rows, width), BF16),
        ],
        scratch_shapes=[pltpu.VMEM((length, dim), F32), pltpu.VMEM((length, dim), F32)],
        name="aback",
    )(qkv, keys, keys, go, qid_row, kid_col)


def heads_back_body(dq, own, got, raw, cos, sin, gq, gk, out, sums, *, heads, kv_heads, dim):
    @pl.when(pl.program_id(0) == 0)
    def _():
        sums[...] = jnp.zeros_like(sums)

    cosine = cos[...]
    sine = sin[...]
    dkv = own[...] + got[...].astype(F32)
    for h in range(heads + kv_heads):
        is_query = h < heads
        g = dq[:, h * dim : (h + 1) * dim] if is_query else dkv[:, (h - heads) * dim : (h - heads + 1) * dim]
        gain = (gq if is_query else gk)[...].astype(F32)
        v = raw[:, h * dim : (h + 1) * dim]
        r = lax.rsqrt(jnp.mean(v * v, axis=-1, keepdims=True) + EPS)
        unit = v * r
        gn = g * cosine + pltpu.roll(g * sine, dim // 2, axis=1)
        line = 0 if is_query else 1
        sums[line : line + 1, :] += jnp.sum(gn * unit, axis=0, keepdims=True)
        e = gn * gain
        back = r * (e - unit * jnp.mean(e * unit, axis=-1, keepdims=True))
        out[:, h * dim : (h + 1) * dim] = back.astype(BF16)
    out[:, (heads + kv_heads) * dim :] = dkv[:, kv_heads * dim :].astype(BF16)


def heads_back(dq, own, got, raw, cos, sin, gq, gk, heads, kv_heads, dim):
    rows = dq.shape[0]
    block = min(256, rows)
    width = (heads + 2 * kv_heads) * dim
    row = lambda cols: pl.BlockSpec((block, cols), lambda i: (i, 0))
    full = lambda a: pl.BlockSpec(a.shape, lambda i: (0, 0))
    return pl.pallas_call(
        functools.partial(heads_back_body, heads=heads, kv_heads=kv_heads, dim=dim),
        grid=(rows // block,),
        in_specs=[row(a.shape[1]) for a in (dq, own, got, raw, cos, sin)] + [full(gq), full(gk)],
        out_specs=[row(width), pl.BlockSpec((8, dim), lambda i: (0, 0))],
        out_shape=[shape(rows, width, BF16), shape(8, dim, F32)],
        name="hback",
    )(dq, own, got, raw, cos, sin, gq, gk)


def shards(
    tokens,
    positions,
    block_ids,
    attn_gain,
    w_query,
    w_key,
    w_value,
    w_out,
    query_gain,
    key_gain,
    mlp_gain,
    w_gate,
    w_up,
    w_down,
    cotangent,
    *,
    sizes,
):
    dp_n, ctx_n, tp_n = sizes
    dp_at, ctx_at, tp_at = (lax.axis_index(name) for name in ("dp", "ctx", "tp"))
    batch, shard_len, model = tokens.shape
    rows = batch * shard_len
    quarter = rows // tp_n
    dim = query_gain.shape[0]
    heads = w_query.shape[1] // dim
    kv_heads = w_key.shape[1] // dim
    piece = w_query.shape[0]
    attn_width = w_query.shape[1]
    own_width = dp_n * piece
    places = dp_n * ctx_n
    aligned = piece % 128 == 0

    place = jnp.arange(places, dtype=jnp.int32)
    dp_of = lax.rem(dp_at + 2 * dp_n - 1 - lax.rem(place, dp_n), dp_n)
    ctx_of = lax.rem(ctx_at + ctx_n - place // dp_n, ctx_n)
    to_local_at = dp_of * ctx_n + ctx_of
    place_dp, place_ctx = place // ctx_n, lax.rem(place, ctx_n)
    back_j = lax.rem(dp_at + 2 * dp_n - 1 - place_dp, dp_n)
    to_global_at = lax.rem(ctx_at + ctx_n - place_ctx, ctx_n) * dp_n + back_j

    bits = []
    while (1 << len(bits)) < tp_n:
        bits.append(1 << len(bits))
    masks = [0]
    for bit in reversed(bits):
        masks = masks + [mask | bit for mask in masks]
    rank = jnp.bitwise_xor(tp_at, jnp.array(masks, jnp.int32)).astype(jnp.int32)
    owner = sum((rank // bit % 2) * (tp_n // (2 * bit)) for bit in bits)

    def columns(value, at, row_at=None):
        if row_at is None:
            row_at = jnp.arange(2, dtype=jnp.int32)
        row_blocks = row_at.shape[0]
        if aligned:
            return reorder(value, jnp.concatenate([row_at, at]), row_blocks, piece)
        block = value.shape[0] // row_blocks
        value = jnp.concatenate(
            [lax.dynamic_slice_in_dim(value, row_at[i] * block, block, 0) for i in range(row_blocks)]
        )
        return jnp.concatenate(
            [lax.dynamic_slice_in_dim(value, at[i] * piece, piece, 1) for i in range(places)], axis=1
        )

    def own_order(value):
        parts = value.reshape(tp_n, quarter)
        parts = [lax.dynamic_slice_in_dim(parts, owner[i], 1, 0) for i in range(tp_n)]
        return jnp.concatenate(parts, axis=1).reshape(value.shape)

    def send(value, axis, swap=0):
        size = {"dp": dp_n, "ctx": ctx_n, "tp": tp_n}[axis]
        pairs = [(i, i ^ swap) for i in range(size)] if swap else ring(size)
        return lax.ppermute(value, axis, pairs)

    def spread(name, own):
        got, held = {}, own
        if name in CTX_FIRST:
            for t in range(ctx_n):
                if t:
                    held = send(held, "ctx")
                side = held
                for s in range(dp_n):
                    if s:
                        side = send(side, "dp")
                    got[t, (s + dp_n - 1) % dp_n] = side
        else:
            for s in range(dp_n):
                if s:
                    held = send(held, "dp")
                side = held
                for t in range(ctx_n):
                    if t:
                        side = send(side, "ctx")
                    got[t, (s + dp_n - 1) % dp_n] = side
        return [got[t, j] for t in range(ctx_n) for j in range(dp_n)]

    gains = jnp.concatenate([attn_gain, mlp_gain])
    first_pack = jnp.concatenate([w_query, w_key, w_value], axis=1)
    gain_row = jnp.pad(gains[None, :], ((0, 7), (0, first_pack.shape[1] - gains.shape[0])))
    firsts = spread("q", jnp.concatenate([first_pack, gain_row], axis=0))
    outs = spread("o", w_out.T)
    gates = spread("g", w_gate)
    uppers = spread("u", w_up)
    downs = spread("d", w_down)
    gain_one = jnp.concatenate([a[piece : piece + 1, :piece] for a in firsts], axis=1)
    gain_two = jnp.concatenate([a[piece : piece + 1, piece : 2 * piece] for a in firsts], axis=1).astype(F32)
    step = piece
    if not aligned:
        firsts = [jnp.concatenate([a[:piece] for a in firsts])]
        step = model
    qkv_w, out_w = joined([a[:step] for a in firsts]), joined(outs)
    gate_w, up_w, down_w = joined(gates), joined(uppers), joined(downs, 1)

    def fold(function, *operands):
        total = function(*operands).astype(BF16)
        for bit in bits:
            half = total.shape[0] // 2
            got = send(total[half:].astype(BF16), "tp", swap=bit)
            total = total[:half].astype(F32) + got.astype(F32)
        return total

    def unfold(own):
        held = [(0, own)]
        for bit in reversed(bits):
            held = held + [(mask | bit, send(value, "tp", swap=bit)) for mask, value in held]
        return [value for _, value in held]

    def assemble(quarters, dtype):
        whole = jnp.zeros((rows, model), dtype)
        for k, value in enumerate(quarters):
            whole = lax.dynamic_update_slice_in_dim(whole, value.astype(dtype), owner[k] * quarter, 0)
        return whole.reshape(batch, shard_len, model)

    flat_tokens = columns(tokens.reshape(rows, model), to_local_at, owner)
    ids = own_order(block_ids)
    cot = columns(cotangent.reshape(rows, model), to_local_at, owner)
    exponent = jnp.arange(dim // 2, dtype=F32) * (2.0 / dim)
    angle = own_order(positions).reshape(rows, 1).astype(F32) * jnp.power(THETA, -exponent)[None, :]
    cosine, sine = jnp.cos(angle), jnp.sin(angle)
    cosine = jnp.concatenate([cosine, cosine], axis=1)
    sine = jnp.concatenate([-sine, sine], axis=1)
    gain_q, gain_k = query_gain[None, :], key_gain[None, :]

    def around(value):
        held = [value]
        for _ in range(1, ctx_n):
            held.append(send(held[-1], "ctx"))
        return jnp.concatenate(held, axis=1)

    key_ids = around(ids)
    normed, raw, qkv = project(
        owner, flat_tokens, gain_one, cosine, sine, gain_q, gain_k, firsts, step, heads, kv_heads, dim
    )
    qkv = qkv.reshape(batch, shard_len, -1)
    keys = around(qkv[:, :, attn_width:])
    attended = attend(qkv, keys, ids[:, :, None], key_ids[:, None, :], heads, kv_heads, dim)
    attended = attended.reshape(rows, attn_width)
    branch = fold(against, attended, out_w)
    own_tokens = flat_tokens[:quarter].astype(F32)
    hidden = own_tokens + branch

    root_two = lax.rsqrt(jnp.mean(hidden * hidden, axis=-1, keepdims=True) + EPS)
    unit_two = hidden * root_two
    normed_two = joined(unfold((unit_two * gain_two).astype(BF16)))
    gate = lax.optimization_barrier(matmul(normed_two, gate_w).astype(BF16))
    upper = matmul(normed_two, up_w)
    wide = gate.astype(F32)
    active = (wide * jax.nn.sigmoid(wide) * upper).astype(BF16)
    gate, upper, active = lax.optimization_barrier((gate, upper.astype(BF16), active))

    def share(name, left, right, rows_split):
        axis = 0 if rows_split else 1
        model_side = left if rows_split else right

        def part(start, width):
            cut = lax.slice_in_dim(model_side, start, start + width, axis=1)
            return (over_rows(cut, right) if rows_split else over_rows(left, cut)).astype(BF16)

        def block(value, start):
            return lax.slice_in_dim(value, start, start + piece, axis=axis).astype(F32)

        keep = part(0, own_width)
        if name in DP_FIRST:
            totals = []
            for t in range(ctx_n):
                side = part(t * own_width, own_width) if t else keep
                total = None
                for j in range(dp_n):
                    value = block(side, j * piece)
                    if total is not None:
                        value = value + send(total.astype(BF16), "dp").astype(F32)
                    total = value
                totals.append(total)
            held = totals[1 % ctx_n]
            for t in range(1, ctx_n):
                held = totals[(t + 1) % ctx_n] + send(held.astype(BF16), "ctx").astype(F32)
            return held
        half = own_width // 2
        held = None
        for t in range(1, ctx_n):
            new = [part(t * own_width + h * half, half) for h in range(2)]
            if held is not None:
                new = [(a.astype(F32) + b.astype(F32)).astype(BF16) for a, b in zip(held, new)]
            held = [send(value, "ctx") for value in new]
        total = None
        for j in range(dp_n):
            value = block(keep, j * piece)
            if held is not None:
                start = j * piece
                value = value + block(held[start // half], start % half)
            if total is not None:
                value = value + send(total.astype(BF16), "dp").astype(F32)
            total = value
        return total

    grad_down = share("D", active, cot, False)
    g_active = against(cot, down_w)
    wide = gate.astype(F32)
    sigmoid = jax.nn.sigmoid(wide)
    g_gate = (g_active * upper.astype(F32) * sigmoid * (1.0 + wide * (1.0 - sigmoid))).astype(BF16)
    g_up = (g_active * (wide * sigmoid)).astype(BF16)
    g_normed_two = fold(lambda a, b, w, v: against(a, w) + against(b, v), g_gate, g_up, gate_w, up_w)
    grad_gate = share("G", normed_two, g_gate, True)
    grad_up = share("U", normed_two, g_up, True)
    result = (hidden + fold(matmul, active, down_w)).astype(BF16)
    layer_output = assemble(unfold(columns(result, to_global_at)), BF16)
    e_two = g_normed_two * gain_two
    g_hidden = cot[:quarter].astype(F32) + root_two * (
        e_two - unit_two * jnp.mean(e_two * unit_two, axis=-1, keepdims=True)
    )
    mlp_gain_sum = jnp.sum(g_normed_two * unit_two, axis=0)

    g_branch = joined(unfold(g_hidden.astype(BF16)))
    g_attended = matmul(g_branch, out_w).astype(BF16)
    grad_out = share("O", attended, g_branch, False)
    dq, own, other = attend_back(
        qkv,
        keys,
        g_attended.reshape(batch, shard_len, attn_width),
        ids[:, None, :],
        key_ids[:, :, None],
        heads,
        kv_heads,
        dim,
    )
    others = [other[:, i * shard_len : (i + 1) * shard_len] for i in range(ctx_n - 1)]
    got = others[0]
    for t in range(1, ctx_n):
        got = send(got, "ctx")
        if t < ctx_n - 1:
            got = (others[t].astype(F32) + got.astype(F32)).astype(BF16)
    g_raw, gain_sums = heads_back(
        dq.reshape(rows, attn_width),
        own.reshape(rows, -1),
        got.reshape(rows, -1),
        raw,
        cosine,
        sine,
        gain_q,
        gain_k,
        heads,
        kv_heads,
        dim,
    )
    g_normed = fold(against, g_raw, qkv_w)
    grad_qkv = share("Q", normed, g_raw, True)
    root_one = lax.rsqrt(jnp.mean(own_tokens * own_tokens, axis=-1, keepdims=True) + EPS)
    unit_one = own_tokens * root_one
    e_one = g_normed * gain_one.astype(F32)
    input_own = g_hidden + root_one * (
        e_one - unit_one * jnp.mean(e_one * unit_one, axis=-1, keepdims=True)
    )
    input_grad = assemble(unfold(columns(input_own.astype(BF16), to_global_at)), F32)
    attn_gain_sum = jnp.sum(g_normed * unit_one, axis=0)

    chosen = (to_global_at[:, None] == place[None, :]).astype(F32)

    def whole_order(vector):
        blocks = vector.reshape(places, piece)
        return jnp.sum(chosen[:, :, None] * blocks[None, :, :], axis=1).reshape(model)

    small = jnp.concatenate(
        [whole_order(mlp_gain_sum), whole_order(attn_gain_sum), gain_sums[0], gain_sums[1]]
    ).reshape(-1, dim)
    for name, size in (("tp", tp_n), ("ctx", ctx_n), ("dp", dp_n)):
        bit = 1
        while bit < size:
            small = small + send(small, name, swap=bit)
            bit *= 2
    small = small.reshape(-1)
    start = (dp_at * ctx_n + ctx_at) * piece
    grad_mlp_gain = lax.dynamic_slice_in_dim(small, start, piece, 0)
    grad_attn_gain = lax.dynamic_slice_in_dim(small, model + start, piece, 0)
    grad_query_gain = small[2 * model : 2 * model + dim]
    grad_key_gain = small[2 * model + dim :]

    kv_width = kv_heads * dim
    return (
        layer_output,
        input_grad,
        grad_attn_gain,
        grad_qkv[:, :attn_width],
        grad_qkv[:, attn_width : attn_width + kv_width],
        grad_qkv[:, attn_width + kv_width :],
        grad_out,
        grad_query_gain,
        grad_key_gain,
        grad_mlp_gain,
        grad_gate,
        grad_up,
        grad_down,
    )


def solution(mesh):
    rows_split = P(("dp", "ctx"), "tp")
    cols_split = P("tp", ("dp", "ctx"))
    vector = P(("dp", "ctx"))
    tokens = P("dp", "ctx", None)
    sizes = tuple(mesh.shape[name] for name in ("dp", "ctx", "tp"))

    def body(*arrays):
        return shards(*arrays, sizes=sizes)

    return jax.shard_map(
        body,
        mesh=mesh,
        in_specs=(
            tokens,
            P("dp", "ctx"),
            P("dp", "ctx"),
            vector,
            rows_split,
            rows_split,
            rows_split,
            cols_split,
            P(),
            P(),
            vector,
            rows_split,
            rows_split,
            cols_split,
            tokens,
        ),
        out_specs=(
            tokens,
            tokens,
            vector,
            rows_split,
            rows_split,
            rows_split,
            cols_split,
            P(),
            P(),
            vector,
            rows_split,
            rows_split,
            cols_split,
        ),
        check_vma=False,
    )
```
